256 devices in a mesh: sector: 8 (over x, core), section: 32 (over z, y).
Axes of the slice: x: 4, y: 4, z: 8, core: 2. Of those that a mesh axis runs over, the one named last changes fastest.
Arguments:
- vectors: bfloat16 [98304, 512], P(('sector', 'section')), may hold values from -6 to 6
- sectors: int32 [98304, 2], P(('sector', 'section')), may hold values from 0 to 31, all different within a row; in each aligned block of 384 rows (0 to 383, 384 to 767, ...) at most 36 rows name the same one
- outcomes: int32 [98304, 2], P(('sector', 'section')), may hold values from 0 to 3
- sites: bfloat16 [2, 32, 512, 2048], P(None, 'sector'), may hold values from -0.25 to 0.25
- environments: bfloat16 [2, 32, 4, 512, 512], P(None, 'sector', None, 'section'), may hold values from -100 to 150, as said below
Outputs:
- probabilities: bfloat16 [98304, 8], P(('sector', 'section'))
- final_vectors: bfloat16 [98304, 512], P(('sector', 'section'))
The draws below stay inside these ranges and needn't reach their ends.
Inputs may be any that keep to these rules, and one draw needn't show every extreme that they name: `sectors`: in the rows of one device no sector appears more than 36 times over all orbitals together, and on some device some sector appears exactly 36 times. Every block environments[k, q, s] is symmetric and positive definite.
All inputs are finite; a program needn't handle non-finite values.
Results may differ from the reference program's by a relative error of at most 0.0049.
Values may be sent and summed in bfloat16 or wider, within the bound.
No kernel may reach another device: no remote copies, remote signals or barrier semaphores. Data moves between devices by JAX's collectives and lax.ppermute only.
A program may use at most 128 MiB of HBM per device.

```python
import math
import jax
import jax.numpy as jnp
import numpy as np
from jax import lax

B = 512
OUTCOMES = 4
ORBITALS = 2
SMP_DEV = 384
NSEC = 32
SAMPLES = 98304
CAP = 36


def draw_environments(key, part):
    key_dense = jax.random.fold_in(key, 11)
    key_scale = jax.random.fold_in(key, 13)
    shape = (ORBITALS, NSEC, OUTCOMES, B, B)
    index = jnp.arange(B)
    dense = jax.random.normal(key_dense, shape, jnp.float32)
    dense = jnp.where((index == 1)[:, None], -dense[..., 0:1, :], dense)
    dense = dense / jnp.sqrt(jnp.sum(dense * dense, axis=-1, keepdims=True))
    core = jnp.einsum('...ij,...kj->...ik', dense, dense, precision=lax.Precision.HIGHEST)
    identity = (index[:, None] == index[None, :]).astype(jnp.float32)
    core = core + 0.5 * identity
    top_level = 0.5 * math.log(10.0)
    levels = jax.random.uniform(key_scale, shape[:-1], jnp.float32, 0.0, top_level)
    levels = jnp.where(index < 2, top_level, levels)
    spread = jnp.exp(levels)
    return (spread[..., :, None] * core * spread[..., None, :]).astype(jnp.bfloat16)


def set_ends(entries, key, smallest, largest):
    place = [jax.random.randint(jax.random.fold_in(key, axis), (), 0, length) for axis, length in enumerate(entries.shape)]
    main_axis = entries.shape.index(max(entries.shape))
    next_to = place[:main_axis] + [(place[main_axis] + 1) % entries.shape[main_axis]] + place[main_axis + 1:]
    return entries.at[tuple(place)].set(smallest).at[tuple(next_to)].set(largest)


def block_scale(rng, shape, split, low, largest):
    factor_of = 1.0
    for dim, blocks in split:
        draws = jax.random.uniform(jax.random.fold_in(jax.random.fold_in(rng, 6), dim), (blocks,), jnp.float32, low / len(split), largest / len(split))
        factor_of = factor_of * jnp.repeat(jnp.exp(draws), shape[dim] // blocks).reshape((-1,) + (1,) * (len(shape) - 1 - dim))
    return factor_of


def shared_out(key, own, number, rows, count, top, bound, lean):
    sequence = jax.random.permutation(key, count)
    crowded, ordinary = shares(count, rows * top, bound, lean, True), shares(count, rows * top, bound, lean, False)
    places = jnp.arange(count)

    def named(lengths, offset_by):
        used = int((lengths > 0).sum())
        fixed = max(1, used // 4)
        moved = fixed + (places - fixed + offset_by * (used - fixed)) % max(1, count - fixed)
        return jnp.zeros((count,), jnp.int32).at[sequence[jnp.where(places < fixed, places, moved)]].set(jnp.asarray(lengths, jnp.int32))

    lengths = jnp.where(number % 4 == 0, named(crowded, number // 4), named(ordinary, number - number // 4 - 1))
    mixed = jax.random.permutation(jax.random.fold_in(own, 3), count)
    donor, receiver = mixed[0:count // 2 * 2:2], mixed[1:count // 2 * 2:2]
    margin = jnp.minimum(lengths[donor] - 1, bound - lengths[receiver]) // 2
    margin = jnp.where((donor == sequence[0]) | (receiver == sequence[0]) | (lengths[receiver] == 0), 0, jnp.maximum(margin, 0))
    moved = jax.random.randint(jax.random.fold_in(own, 4), (count // 2,), 0, 1 << 20) % (margin + 1)
    lengths = lengths.at[donor].add(-moved).at[receiver].add(moved)
    items = jnp.searchsorted(jnp.cumsum(lengths), jnp.arange(rows * top), side="right").astype(jnp.int32)
    listing = items.reshape(top, rows).T
    listing = listing[jax.random.permutation(jax.random.fold_in(own, 1), rows)]
    offset_by = jax.random.randint(jax.random.fold_in(own, 2), (rows, 1), 0, top)
    return jnp.take_along_axis(listing, (jnp.arange(top)[None, :] + offset_by) % top, axis=1)


def shares(amount, total, reach, lean, full):
    weights = [(1 << 20) // math.isqrt(standing ** lean) + 1 for standing in range(1, amount + 1)]
    largest = reach if full else min(reach, max(-(-total // amount), total * weights[0] // sum(weights)))
    least = 1 if total - largest >= amount - 1 else 0
    counts, rest = [largest] + [least] * (amount - 1), total - largest - least * (amount - 1)
    while rest > 0:
        movable = [i for i in range(1, amount) if counts[i] < largest] or [i for i in range(1, amount) if counts[i] < reach]
        pool, remaining = sum([weights[i] for i in movable]), rest
        for i in movable:
            addition = min(reach - counts[i], max(1, remaining * weights[i] // pool), rest)
            counts[i] = counts[i] + addition
            rest = rest - addition
    return np.array(counts)


def gaussian(own_key, dims, deviation, most, cuts=(), kind=jnp.bfloat16):
    drawn = deviation * jax.random.normal(own_key, dims, jnp.float32)
    if cuts:
        drawn = drawn * block_scale(own_key, dims, cuts, -0.22, 0.18)
    return jnp.clip(drawn, -most, most).astype(kind)


def setup_inputs(seed: int = 0) -> dict:
    keys = jax.random.split(jax.random.key(seed), 6)
    vectors = gaussian(keys[0], (SAMPLES, B), 1.0, 6.0, ((0, 256),))
    sectors_keys = jax.random.split(jax.random.fold_in(keys[1], 1), SAMPLES // SMP_DEV)
    sectors_turns = jax.random.permutation(jax.random.fold_in(keys[1], 3), SAMPLES // SMP_DEV)
    sectors = jax.vmap(lambda own, number: shared_out(jax.random.fold_in(keys[1], 2), own, number, SMP_DEV, NSEC, ORBITALS, CAP, 2))(sectors_keys, sectors_turns).reshape((SAMPLES, ORBITALS))
    outcomes = set_ends(jax.random.randint(keys[2], (SAMPLES, ORBITALS), 0, OUTCOMES), jax.random.fold_in(keys[2], 1), 0, OUTCOMES - 1).astype(jnp.int32)
    sites = gaussian(keys[3], (ORBITALS, NSEC, B, OUTCOMES * B), B ** -0.5, 0.25, ((1, 8),))
    environments = draw_environments(jax.random.fold_in(keys[5], 71), 0)
    return dict(vectors=vectors, sectors=sectors, outcomes=outcomes, sites=sites, environments=environments)


def orbital_pass(current, labels, chosen_ids, site_k, environ_k):
    sample_total = labels.shape[0]
    block_size = math.gcd(sample_total, 256)
    block_count = sample_total // block_size
    ordering = jnp.argsort(labels, stable=True).astype(jnp.int32)
    sorted_labels = labels[ordering]
    sorted_rows = current[ordering]
    sorted_ids = chosen_ids[ordering]

    def process_block(pieces):
        block_rows, block_labels, block_ids = pieces
        lowest = block_labels[0]
        highest = block_labels[-1]
        start_pair = (jnp.zeros((block_size, OUTCOMES), jnp.bfloat16), jnp.zeros((block_size, B), jnp.bfloat16))

        def sector_step(sector_id, carry_pair):
            amplitudes = jnp.dot(block_rows, site_k[sector_id], preferred_element_type=jnp.float32)
            amplitudes = amplitudes.reshape(block_size, OUTCOMES, B)
            rounded = lax.optimization_barrier(amplitudes.astype(jnp.bfloat16)).astype(jnp.float32)
            images = jnp.einsum('rsb,sbe->rse', rounded, environ_k[sector_id].astype(jnp.float32))
            weights = lax.optimization_barrier(jnp.sum(images * amplitudes, axis=-1))
            norm_sum = lax.optimization_barrier(jnp.sum(weights, axis=-1))
            branch_probs = (weights / norm_sum[:, None]).astype(jnp.bfloat16)
            chosen_mask = (block_ids[:, None] == jnp.arange(OUTCOMES, dtype=jnp.int32)[None, :]).astype(jnp.float32)
            chosen_weight = lax.optimization_barrier(jnp.sum(chosen_mask * weights, axis=-1))
            picked = lax.optimization_barrier(jnp.sum(chosen_mask[:, :, None] * amplitudes, axis=1))
            advanced = (picked * lax.rsqrt(chosen_weight / B)[:, None]).astype(jnp.bfloat16)
            inside = (block_labels == sector_id)[:, None]
            return (jnp.where(inside, branch_probs, carry_pair[0]), jnp.where(inside, advanced, carry_pair[1]))
        return lax.fori_loop(lowest, highest + 1, sector_step, start_pair)
    probs_sorted, rows_sorted = lax.map(process_block, (sorted_rows.reshape(block_count, block_size, B), sorted_labels.reshape(block_count, block_size), sorted_ids.reshape(block_count, block_size)))
    branch_probs = jnp.zeros((sample_total, OUTCOMES), jnp.bfloat16).at[ordering].set(probs_sorted.reshape(sample_total, OUTCOMES))
    advanced = jnp.zeros((sample_total, B), jnp.bfloat16).at[ordering].set(rows_sorted.reshape(sample_total, B))
    return (branch_probs, advanced)

def reference(vectors, sectors, outcomes, sites, environments):
    current = vectors
    columns = []
    for orbital in range(ORBITALS):
        branch_probs, current = orbital_pass(current, sectors[:, orbital], outcomes[:, orbital], sites[orbital], environments[orbital])
        columns.append(branch_probs)
    return (jnp.concatenate(columns, axis=1), current)
```

```python
import functools

import jax
import jax.numpy as jnp
from jax import lax
from jax.experimental import pallas as pl
from jax.experimental.pallas import tpu as pltpu
from jax.sharding import Mesh
from jax.sharding import PartitionSpec as P

OUTCOMES = 4
ORBITALS = 2
CAP = 36
MSG = 40
VMEM_LIMIT = 56 * 1024 * 1024

F32 = jnp.float32
BF16 = jnp.bfloat16


def vmem_specs(number):
    return [pl.BlockSpec(memory_space=pltpu.VMEM)] * number


def call(body, outs, *args, scratch=()):
    return pl.pallas_call(
        body,
        out_shape=outs,
        in_specs=vmem_specs(len(args)),
        out_specs=jax.tree.map(lambda _: pl.BlockSpec(memory_space=pltpu.VMEM), outs),
        scratch_shapes=list(scratch),
        compiler_params=pltpu.CompilerParams(vmem_limit_bytes=VMEM_LIMIT),
    )(*args)


def iota(shape, dim):
    return lax.broadcasted_iota(jnp.int32, shape, dim)


def mm(a, b):
    return jnp.dot(a, b, preferred_element_type=F32)


def as_bf16(mask):
    return jnp.where(mask, 1.0, 0.0).astype(BF16)


def column_ranks(labels):
    n = labels.shape[0]
    onehot = jnp.where(iota((n, 128), 1) == labels, 1.0, 0.0)
    earlier = as_bf16(iota((n, n), 1) < iota((n, n), 0))
    return jnp.sum(mm(earlier, onehot.astype(BF16)) * onehot, axis=1, keepdims=True).astype(
        jnp.int32
    )


def row_ranks(labels):
    n = labels.shape[1]
    onehot = jnp.where(iota((128, n), 0) == labels, 1.0, 0.0)
    earlier = as_bf16(iota((n, n), 0) < iota((n, n), 1))
    return jnp.sum(mm(onehot.astype(BF16), earlier) * onehot, axis=0, keepdims=True).astype(
        jnp.int32
    )


def filled_messages(rows, labels_row, ranks_row, ranks_col, codes_col, slots):
    n = rows.shape[0]
    place = as_bf16(iota((slots, n), 0) == labels_row * MSG + ranks_row)
    heads = as_bf16(iota((slots, n), 0) == labels_row * MSG + CAP)
    codes = jnp.where(iota((n, 128), 1) == ranks_col, codes_col, 0.0).astype(BF16)
    return mm(place, rows), mm(heads, codes)


def first_kernel(vec_ref, sec_ref, sect_ref, out_ref, send_ref, ranks_ref, ranks_row_ref):
    slots = send_ref.shape[0]
    sec, sect = sec_ref[...], sect_ref[...]
    cols = [column_ranks(sec[:, k : k + 1]) for k in range(ORBITALS)]
    rows = [row_ranks(sect[k : k + 1, :]) for k in range(ORBITALS)]
    codes = (out_ref[:, 0:1] + 1).astype(F32)
    data, heads = filled_messages(vec_ref[...], sect[0:1, :], rows[0], cols[0], codes, slots)
    send_ref[...] = data.astype(BF16)
    send_ref[:, 0:128] = (data[:, 0:128] + heads).astype(BF16)
    ranks_ref[...] = jnp.concatenate(cols, axis=1)
    ranks_row_ref[...] = jnp.concatenate(rows, axis=0)


def gathered_probs(back, labels_col, ranks_col, slots):
    n = labels_col.shape[0]
    lanes = back[:, 0:128]
    found = []
    for s in range(OUTCOMES):
        pick = as_bf16(iota((n, slots), 1) == labels_col * MSG + (CAP + s))
        line = mm(pick, lanes)
        found.append(
            jnp.sum(jnp.where(iota((n, 128), 1) == ranks_col, line, 0.0), axis=1, keepdims=True)
        )
    return found


def middle_kernel(back_ref, sec_ref, sect_ref, out_ref, ranks_ref, ranks_row_ref, send_ref):
    slots, n = back_ref.shape[0], sec_ref.shape[0]
    pick = as_bf16(iota((n, slots), 1) == sec_ref[:, 0:1] * MSG + ranks_ref[:, 0:1])
    current = mm(pick, back_ref[...]).astype(BF16)
    codes = (out_ref[:, 1:2] + 1).astype(F32)
    data, heads = filled_messages(
        current, sect_ref[1:2, :], ranks_row_ref[1:2, :], ranks_ref[:, 1:2], codes, slots
    )
    send_ref[...] = data.astype(BF16)
    send_ref[:, 0:128] = (data[:, 0:128] + heads).astype(BF16)


def probs_kernel(back_ref, sec_ref, ranks_ref, probs_ref):
    found = gathered_probs(back_ref[...], sec_ref[:, 0:1], ranks_ref[:, 0:1], back_ref.shape[0])
    probs_ref[...] = jnp.concatenate(found, axis=1).astype(BF16)


def last_kernel(back_ref, sec_ref, ranks_ref, probs0_ref, probs_ref, final_ref):
    slots, n = back_ref.shape[0], sec_ref.shape[0]
    back = back_ref[...]
    pick = as_bf16(iota((n, slots), 1) == sec_ref[:, 1:2] * MSG + ranks_ref[:, 1:2])
    final_ref[...] = mm(pick, back).astype(BF16)
    found = gathered_probs(back, sec_ref[:, 1:2], ranks_ref[:, 1:2], slots)
    probs_ref[:, 0:OUTCOMES] = probs0_ref[...]
    probs_ref[:, OUTCOMES : 2 * OUTCOMES] = jnp.concatenate(found, axis=1).astype(BF16)


def pack_kernel(at_ref, env_ref, packed_ref):
    twice = jnp.where(pl.program_id(0) == 1, 2.0, 1.0)
    packed_ref[...] = jnp.swapaxes(env_ref[...].astype(F32) * twice, 0, 1).astype(BF16)


def packed_environments(env, at):
    ks, qs, ss, rs, cs = env.shape
    tile = cs // 4
    return pl.pallas_call(
        pack_kernel,
        out_shape=jax.ShapeDtypeStruct((qs, ks, ss, rs, 3 * tile), BF16),
        grid_spec=pltpu.PrefetchScalarGridSpec(
            num_scalar_prefetch=1,
            grid=(3,),
            in_specs=[
                pl.BlockSpec(
                    (ks, qs, ss, rs, tile), lambda t, at: (0, 0, 0, 0, lax.rem(at[0] + t, 4))
                )
            ],
            out_specs=pl.BlockSpec((qs, ks, ss, rs, tile), lambda t, at: (0, 0, 0, 0, t)),
        ),
    )(at, env)


def stage_kernel(rows_ref, site_ref, packed_ref, back_ref, env_ref, picked_ref):
    width = rows_ref.shape[1]
    tile = width // 4
    chunk = 8 * MSG
    per = packed_ref.shape[0] // 4
    zero = jnp.zeros((tile, tile), BF16)
    for s in range(OUTCOMES):
        for i in range(4):
            own = packed_ref[per * i : per * (i + 1), s].reshape(tile, 3 * tile)
            for t in range(3):
                j = (i + t) % 4
                env_ref[s, tile * i : tile * (i + 1), tile * j : tile * (j + 1)] = own[
                    :, tile * t : tile * (t + 1)
                ]
            j = (i + 3) % 4
            env_ref[s, tile * i : tile * (i + 1), tile * j : tile * (j + 1)] = zero

    def message_of(index):
        return jnp.floor((index.astype(F32) + 0.5) * (1.0 / MSG)).astype(jnp.int32)

    square = (chunk, chunk)
    across, down = iota(square, 1), iota(square, 0)
    head = message_of(down) * MSG + CAP
    spread = as_bf16(across == head)
    sub = iota((chunk, 128), 0)
    within = sub - message_of(sub) * MSG
    diagonal = iota((chunk, 128), 1) == within
    head_t = message_of(across) * MSG + CAP
    rises = [as_bf16(down == head_t + s) for s in range(OUTCOMES)]
    in_data = within[:, 0:1] < CAP

    def step(number, carry):
        at = pl.ds(pl.multiple_of(number * chunk, chunk), chunk)
        rows = rows_ref[at, :]
        code = jnp.sum(
            jnp.where(diagonal, mm(spread, rows[:, 0:128]), 0.0), axis=1, keepdims=True
        )
        code = jnp.where(in_data, code, 0.0)
        weights = []
        for s in range(OUTCOMES):
            amplitudes = mm(rows, site_ref[:, width * s : width * (s + 1)])
            images = mm(amplitudes.astype(BF16), env_ref[s])
            weights.append(jnp.sum(images * amplitudes, axis=1, keepdims=True))
            chosen = code == (s + 1.0)
            if s == 0:
                picked_ref[...] = jnp.where(chosen, amplitudes, 0.0)
            else:
                picked_ref[...] = jnp.where(chosen, amplitudes, picked_ref[...])
        filled = code > 0.0
        total = jnp.where(filled, weights[0] + weights[1] + weights[2] + weights[3], 1.0)
        lines = jnp.zeros((chunk, 128), F32)
        chosen_weight = jnp.zeros((chunk, 1), F32)
        for s in range(OUTCOMES):
            prob = jnp.where(filled, weights[s] / total, 0.0)
            lines += mm(rises[s], jnp.where(diagonal, prob, 0.0).astype(BF16))
            chosen_weight = jnp.where(code == (s + 1.0), weights[s], chosen_weight)
        scale = lax.rsqrt(jnp.where(filled, chosen_weight, 1.0) / width)
        picked = picked_ref[...] * scale
        back_ref[at, :] = picked.astype(BF16)
        back_ref[at, 0:128] = (picked[:, 0:128] + lines).astype(BF16)
        return carry

    lax.fori_loop(0, rows_ref.shape[0] // chunk, step, 0)


def local(vectors, sectors, outcomes, sites, environments, holders):
    n, width = vectors.shape
    sector_total = sites.shape[1] * lax.axis_size("sector")
    slots = sector_total * MSG
    mine = lax.axis_index("part")
    shape = functools.partial(jax.ShapeDtypeStruct)

    at = (lax.axis_index("row") * 4 // lax.axis_size("row")).astype(jnp.int32).reshape(1)
    packed = packed_environments(environments, at)
    packed = lax.all_to_all(packed, "part", split_axis=0, concat_axis=0, tiled=True)
    envs = [
        lax.all_gather(packed[:, k], "row", axis=0, tiled=True) for k in range(ORBITALS)
    ]

    flipped = sectors.T
    send, ranks, ranks_row = call(
        first_kernel,
        (
            shape((slots, width), BF16),
            shape((n, ORBITALS), jnp.int32),
            shape((ORBITALS, n), jnp.int32),
        ),
        vectors,
        sectors,
        flipped,
        outcomes,
    )

    def exchanged(messages):
        messages = messages.reshape(sector_total, MSG, width)
        messages = lax.all_to_all(messages, holders, split_axis=0, concat_axis=0, tiled=True)
        return messages.reshape(slots, width)

    def stage(k, messages):
        site = lax.dynamic_index_in_dim(sites[k], mine, 0, keepdims=False)
        return call(
            stage_kernel,
            shape((slots, width), BF16),
            messages,
            site,
            envs[k],
            scratch=(
                pltpu.VMEM((OUTCOMES, width, width), BF16),
                pltpu.VMEM((8 * MSG, width), F32),
            ),
        )

    back = exchanged(stage(0, exchanged(send)))
    send = call(
        middle_kernel, shape((slots, width), BF16), back, sectors, flipped, outcomes, ranks, ranks_row
    )
    probs0 = call(probs_kernel, shape((n, OUTCOMES), BF16), back, sectors, ranks)
    back = exchanged(stage(1, exchanged(send)))
    return call(
        last_kernel,
        (shape((n, ORBITALS * OUTCOMES), BF16), shape((n, width), BF16)),
        back,
        sectors,
        ranks,
        probs0,
    )


def solution(mesh):
    sector, section = mesh.devices.shape

    def whole(vectors, sectors, outcomes, sites, environments):
        parts = sites.shape[1] // sector
        fine = Mesh(
            mesh.devices.reshape(sector, section // parts, parts), ("sector", "row", "part")
        )
        split = P(("sector", "row", "part"), None)
        return jax.shard_map(
            functools.partial(local, holders=("sector", "part")),
            mesh=fine,
            in_specs=(
                split,
                split,
                split,
                P(None, "sector", None, None),
                P(None, "sector", None, ("row", "part"), None),
            ),
            out_specs=(split, split),
            check_vma=False,
        )(vectors, sectors, outcomes, sites, environments)

    return whole
```

```python
import functools

import jax
import jax.numpy as jnp
from jax import lax
from jax.experimental import pallas as pl
from jax.experimental.pallas import tpu as pltpu
from jax.sharding import Mesh
from jax.sharding import PartitionSpec as P

OUTCOMES = 4
ORBITALS = 2
CAP = 36
MSG = 40
LANES = 128
VMEM_LIMIT = 56 * 1024 * 1024

F32 = jnp.float32
BF16 = jnp.bfloat16


def shape(dims, kind):
    return jax.ShapeDtypeStruct(dims, kind)


def near(x):
    return pltpu.with_memory_space_constraint(x, pltpu.VMEM)


def call(body, outs, *args):
    vmem = pl.BlockSpec(memory_space=pltpu.VMEM)
    return pl.pallas_call(
        body,
        out_shape=outs,
        in_specs=[vmem] * len(args),
        out_specs=jax.tree.map(lambda _: vmem, outs),
        compiler_params=pltpu.CompilerParams(vmem_limit_bytes=VMEM_LIMIT),
    )(*[near(x) for x in args])


def iota(dims, dim):
    return lax.broadcasted_iota(jnp.int32, dims, dim)


def mm(a, b):
    return jnp.dot(a, b, preferred_element_type=F32)


def as_bf16(mask, value=1.0):
    return jnp.where(mask, value, 0.0).astype(BF16)


SECTOR, RANK, CODE = 0, 2, 4


def index_table(sectors, outcomes):
    n = sectors.shape[1]
    earlier = as_bf16(iota((n, n), 0) < iota((n, n), 1))
    ranks = []
    for k in range(ORBITALS):
        onehot = jnp.where(iota((LANES, n), 0) == sectors[k : k + 1, :], 1.0, 0.0)
        before = mm(onehot.astype(BF16), earlier)
        ranks.append(jnp.sum(before * onehot, axis=0, keepdims=True))
    return jnp.concatenate(
        [
            sectors.astype(F32),
            *ranks,
            outcomes.astype(F32) + 1.0,
            jnp.zeros((8 - 3 * ORBITALS, n), F32),
        ],
        axis=0,
    )


def fill_messages(send_ref, rows, k, table, columns):
    slots, n = send_ref.shape[0], rows.shape[0]
    first = table[SECTOR + k : SECTOR + k + 1, :] * MSG
    slot = first + table[RANK + k : RANK + k + 1, :]
    at = iota((slots, n), 0)
    data = mm(as_bf16(at == slot.astype(jnp.int32)), rows)
    send_ref[...] = data.astype(BF16)
    codes = as_bf16(
        iota((n, LANES), 1) == columns[:, RANK + k : RANK + k + 1].astype(jnp.int32),
        columns[:, CODE + k : CODE + k + 1],
    )
    heads = as_bf16(iota((LANES, n), 0) == table[SECTOR + k : SECTOR + k + 1, :].astype(jnp.int32))
    lines = mm(heads, codes)[: slots // MSG]
    in_head = iota((slots // MSG, MSG, LANES), 1) == CAP
    front = data[:, :LANES].reshape(slots // MSG, MSG, LANES)
    front = jnp.where(in_head, lines[:, None, :], front)
    send_ref[:, :LANES] = front.reshape(slots, LANES).astype(BF16)


def picked_rows(back, k, columns):
    slots, n = back.shape[0], columns.shape[0]
    slot = columns[:, SECTOR + k : SECTOR + k + 1] * MSG + columns[:, RANK + k : RANK + k + 1]
    return mm(as_bf16(iota((n, slots), 1) == slot.astype(jnp.int32)), back).astype(BF16)


def picked_probs(back, k, columns):
    slots, n = back.shape[0], columns.shape[0]
    messages = slots // MSG
    front = back[:, :LANES].astype(F32).reshape(messages, MSG, LANES)
    of = as_bf16(
        iota((n, messages), 1) == columns[:, SECTOR + k : SECTOR + k + 1].astype(jnp.int32)
    )
    here = iota((n, LANES), 1) == columns[:, RANK + k : RANK + k + 1].astype(jnp.int32)
    found = []
    for s in range(OUTCOMES):
        lines = mm(of, front[:, CAP + s, :].astype(BF16))
        found.append(jnp.sum(jnp.where(here, lines, 0.0), axis=1, keepdims=True))
    return found


def first_kernel(vec_ref, sec_ref, out_ref, send_ref, table_ref, columns_ref):
    table = index_table(sec_ref[...], out_ref[...])
    columns = table.T
    table_ref[...] = table
    columns_ref[...] = columns
    fill_messages(send_ref, vec_ref[...], 0, table, columns)


def middle_kernel(back_ref, table_ref, columns_ref, send_ref):
    columns = columns_ref[...]
    rows = picked_rows(back_ref[...], 0, columns)
    fill_messages(send_ref, rows, 1, table_ref[...], columns)


def probs_kernel(back_ref, columns_ref, probs_ref):
    columns = columns_ref[...]
    found = picked_probs(back_ref[...], 0, columns)
    probs_ref[...] = jnp.concatenate(found + found, axis=1)


def last_kernel(back_ref, columns_ref, probs0_ref, probs_ref, final_ref):
    columns, back = columns_ref[...], back_ref[...]
    final_ref[...] = picked_rows(back, 1, columns)
    found = jnp.concatenate(picked_probs(back, 1, columns), axis=1)
    both = jnp.concatenate([probs0_ref[:, :OUTCOMES], found], axis=1)
    probs_ref[...] = both.T.astype(BF16)


def pack_kernel(place_ref, first_ref, second_ref, rest_ref, *packed_refs):
    ks, qs, ss, rs, lanes = first_ref.shape
    odd = lax.rem(place_ref[0], 2) == 1
    lane = iota((ss, rs, lanes), 2)
    low = lane < lanes // 2
    first_weight = jnp.where(low & jnp.logical_not(odd), 1.0, 2.0)
    second_weight = jnp.where(low | jnp.logical_not(odd), 2.0, 1.0)
    for d in range(qs):
        q = lax.rem(place_ref[1] + d, qs)
        for k in range(ks):
            parts = [
                (first_ref[k, q].astype(F32) * first_weight).reshape(ss * rs, lanes),
                (second_ref[k, q].astype(F32) * second_weight).reshape(ss * rs, lanes),
            ]
            rest = rest_ref[k, q].astype(F32)
            for s in range(0, ss, 2):
                one, two = rest[s], rest[s + 1]
                one = jnp.where(odd, pltpu.roll(one, lanes // 2, 1), one)
                two = jnp.where(odd, two, pltpu.roll(two, lanes // 2, 1))
                parts.append(jnp.where(low[0], one, two))
            packed_refs[d][k] = jnp.concatenate(parts, axis=0).astype(BF16)


def packed_blocks(place, environments):
    ks, qs, ss, rs, cs = environments.shape
    line = (ks, 10 * rs, LANES)
    tile = (ks, qs, ss, rs, LANES)

    def at(index):
        return pl.BlockSpec(tile, lambda i, place: (0, 0, 0, 0, lax.rem(index(place[0]), 4)))

    return pl.pallas_call(
        pack_kernel,
        out_shape=[shape(line, BF16)] * qs,
        grid_spec=pltpu.PrefetchScalarGridSpec(
            num_scalar_prefetch=1,
            grid=(1,),
            in_specs=[
                at(lambda z: lax.div(z + 1, 2)),
                at(lambda z: lax.div(z + 1, 2) + 1),
                at(lambda z: lax.div(z, 2) + 2 - 2 * lax.rem(z, 2)),
            ],
            out_specs=[pl.BlockSpec(line, lambda i, place: (0, 0, 0))] * qs,
        ),
        compiler_params=pltpu.CompilerParams(vmem_limit_bytes=VMEM_LIMIT),
    )(place, environments, environments, environments)


def unpack(part, blocks, env_ref):
    ds = 4
    rs = env_ref.shape[1] // (8 * ds)
    lane = iota((rs, LANES), 1)
    zero = jnp.zeros((rs, LANES), BF16)
    for z in range(8):
        odd, tile = z % 2, z // 2
        keep = (lane >= LANES // 2) if odd else (lane < LANES // 2)
        for d in range(ds):
            first = z * ds * rs + lax.rem(part + ds - d, ds) * rs
            rows = pl.ds(pl.multiple_of(first, rs), rs)
            block = blocks.at[z, d]

            def put(s, at, value):
                at %= 4
                env_ref[s, rows, at * LANES : (at + 1) * LANES] = value

            for s in range(OUTCOMES):
                put(s, tile + odd, block[s * rs : (s + 1) * rs, :])
                put(s, tile + odd + 1, block[(OUTCOMES + s) * rs : (OUTCOMES + s + 1) * rs, :])
                at = (2 * OUTCOMES + s // 2) * rs
                half = block[at : at + rs, :].astype(F32)
                if s % 2 != odd:
                    half = pltpu.roll(half, LANES // 2, 1)
                put(s, tile if odd else tile + 2, jnp.where(keep, half, 0.0).astype(BF16))
                put(s, tile + 3, zero)


def stage_kernel(count, k, place_ref, rows_ref, sites_hbm, *refs):
    packed_hbm, back_hbm = refs[:count], refs[count]
    packed, site_ref, back_ref, env_ref, picked_ref, in_sems, out_sems = refs[count + 1 :]
    row, part = place_ref[0], place_ref[1]
    slots, width = rows_ref.shape
    chunk = picked_ref.shape[0]
    depth = packed.shape[0]
    if count == 1:
        fetches = [pltpu.make_async_copy(packed_hbm[0], packed, in_sems.at[0])]
    else:
        fetches = [
            pltpu.make_async_copy(
                packed_hbm[i], packed.at[lax.rem(row + depth - i, depth)], in_sems.at[i]
            )
            for i in range(count)
        ]
    fetches.append(pltpu.make_async_copy(sites_hbm.at[k, part], site_ref, in_sems.at[count]))
    for fetch in fetches:
        fetch.start()
    for fetch in fetches[:count]:
        fetch.wait()
    unpack(part, packed, env_ref)
    for fetch in fetches[count:]:
        fetch.wait()

    messages = chunk // MSG
    cube = (messages, MSG, LANES)
    within = iota(cube, 1).reshape(chunk, LANES)
    diagonal = iota((chunk, LANES), 1) == within
    in_data = within[:, 0:1] < CAP
    sent = []
    for number, start in enumerate(range(0, slots, chunk)):
        at = slice(start, start + chunk)
        rows = rows_ref[at, :]
        front = rows[:, :LANES].astype(F32).reshape(cube)
        codes = jnp.broadcast_to(front[:, CAP : CAP + 1, :], cube).reshape(chunk, LANES)
        code = jnp.sum(jnp.where(diagonal, codes, 0.0), axis=1, keepdims=True)
        code = jnp.where(in_data, code, 0.0)
        weights = []
        for s in range(OUTCOMES):
            amplitudes = mm(rows, site_ref[:, width * s : width * (s + 1)])
            images = mm(amplitudes.astype(BF16), env_ref[s])
            weights.append(jnp.sum(images * amplitudes, axis=1, keepdims=True))
            chosen = code == (s + 1.0)
            if s == 0:
                picked_ref[...] = jnp.where(chosen, amplitudes, 0.0)
            else:
                picked_ref[...] = jnp.where(chosen, amplitudes, picked_ref[...])
        filled = code > 0.0
        total = jnp.where(filled, weights[0] + weights[1] + weights[2] + weights[3], 1.0)
        lines = jnp.zeros((chunk, LANES), F32)
        chosen_weight = jnp.ones((chunk, 1), F32)
        for s in range(OUTCOMES):
            prob = jnp.where(filled, weights[s] / total, 0.0)
            line = jnp.sum(jnp.where(diagonal, prob, 0.0).reshape(cube), axis=1, keepdims=True)
            line = jnp.broadcast_to(line, cube).reshape(chunk, LANES)
            lines = jnp.where(within == CAP + s, line, lines)
            chosen_weight = jnp.where(code == (s + 1.0), weights[s], chosen_weight)
        picked = picked_ref[...] * lax.rsqrt(chosen_weight / width)
        back_ref[at, :] = picked.astype(BF16)
        back_ref[at, :LANES] = jnp.where(in_data, picked[:, :LANES], lines).astype(BF16)
        copy = pltpu.make_async_copy(back_ref.at[at], back_hbm.at[at], out_sems.at[number])
        copy.start()
        sent.append(copy)
    for copy in sent:
        copy.wait()


def stage(k, place, rows, sites, packed):
    slots, width = rows.shape
    chunk = 16 * MSG
    count = len(packed)
    block = packed[0].shape[-3:]
    hbm, vmem = pl.BlockSpec(memory_space=pl.ANY), pl.BlockSpec(memory_space=pltpu.VMEM)
    return pl.pallas_call(
        functools.partial(stage_kernel, count, k),
        out_shape=shape((slots, width), BF16),
        in_specs=[pl.BlockSpec(memory_space=pltpu.SMEM), vmem] + [hbm] * (1 + count),
        out_specs=hbm,
        scratch_shapes=[
            pltpu.VMEM((8, *block), BF16),
            pltpu.VMEM(sites.shape[2:], BF16),
            pltpu.VMEM((slots, width), BF16),
            pltpu.VMEM((OUTCOMES, width, width), BF16),
            pltpu.VMEM((chunk, width), F32),
            pltpu.SemaphoreType.DMA((count + 1,)),
            pltpu.SemaphoreType.DMA((slots // chunk,)),
        ],
        compiler_params=pltpu.CompilerParams(vmem_limit_bytes=VMEM_LIMIT),
    )(place, near(rows), sites, *packed)


def local(vectors, sectors, outcomes, sites, environments):
    n, width = vectors.shape
    sector_total = sites.shape[1] * lax.axis_size("sector")
    parts, depth = lax.axis_size("part"), lax.axis_size("row")
    slots = sector_total * MSG
    place = jnp.stack([lax.axis_index("row"), lax.axis_index("part")]).astype(jnp.int32)

    blocks = packed_blocks(place, environments)
    blocks = [blocks[0]] + [
        lax.ppermute(blocks[d], "part", [(i, (i + d) % parts) for i in range(parts)])
        for d in range(1, parts)
    ]
    env0, env1 = (jnp.stack([block[k] for block in blocks]) for k in range(ORBITALS))
    env0, vectors = lax.optimization_barrier((env0, vectors))
    env0 = [lax.all_gather(env0, "row", axis=0)]
    send, table, columns = call(
        first_kernel,
        (shape((slots, width), BF16), pltpu.VMEM((8, n), F32), pltpu.VMEM((n, 8), F32)),
        vectors,
        sectors.T,
        outcomes.T,
    )

    def exchanged(messages):
        messages = messages.reshape(sector_total, MSG, width)
        messages = lax.all_to_all(
            messages, ("sector", "part"), split_axis=0, concat_axis=0, tiled=True
        )
        return messages.reshape(slots, width)

    back = exchanged(send)
    env1, _ = lax.optimization_barrier((env1, env0))
    env1 = [lax.all_gather(env1, "row", axis=0)]
    back = exchanged(stage(0, place, back, sites, env0))
    send = call(middle_kernel, shape((slots, width), BF16), back, table, columns)
    probs0 = call(probs_kernel, pltpu.VMEM((n, 8), F32), back, columns)
    back = exchanged(stage(1, place, exchanged(send), sites, env1))
    probs, final = call(
        last_kernel,
        (shape((ORBITALS * OUTCOMES, n), BF16), shape((n, width), BF16)),
        back,
        columns,
        probs0,
    )
    return (probs.T, final)


def solution(mesh):
    sector, section = mesh.devices.shape

    def whole(vectors, sectors, outcomes, sites, environments):
        parts = sites.shape[1] // sector
        fine = Mesh(
            mesh.devices.reshape(sector, section // parts, parts), ("sector", "row", "part")
        )
        split = P(("sector", "row", "part"), None)
        return jax.shard_map(
            local,
            mesh=fine,
            in_specs=(
                split,
                split,
                split,
                P(None, "sector", None, None),
                P(None, "sector", None, ("row", "part"), None),
            ),
            out_specs=(split, split),
            check_vma=False,
        )(vectors, sectors, outcomes, sites, environments)

    return whole
```

```python
import functools

import jax
import jax.numpy as jnp
from jax import lax
from jax.experimental import pallas as pl
from jax.experimental.pallas import tpu as pltpu
from jax.sharding import Mesh
from jax.sharding import PartitionSpec as P

OUTCOMES = 4
ORBITALS = 2
CAP = 36
MSG = 40
LANES = 128
PARTS = 4
VMEM_LIMIT = 56 * 1024 * 1024
PACK_LIMIT = 10 * 1024 * 1024

F32 = jnp.float32
BF16 = jnp.bfloat16


def shape(dims, kind):
    return jax.ShapeDtypeStruct(dims, kind)


def near(x):
    return pltpu.with_memory_space_constraint(x, pltpu.VMEM)


def call(body, outs, *args):
    vmem = pl.BlockSpec(memory_space=pltpu.VMEM)
    return pl.pallas_call(
        body,
        out_shape=outs,
        in_specs=[vmem] * len(args),
        out_specs=jax.tree.map(lambda _: vmem, outs),
        compiler_params=pltpu.CompilerParams(vmem_limit_bytes=VMEM_LIMIT),
    )(*[near(x) for x in args])


def iota(dims, dim):
    return lax.broadcasted_iota(jnp.int32, dims, dim)


def mm(a, b):
    return jnp.dot(a, b, preferred_element_type=F32)


def as_bf16(mask, value=1.0):
    return jnp.where(mask, value, 0.0).astype(BF16)


SECTOR, RANK, CODE = 0, 2, 4


def index_table(sectors, outcomes):
    n = sectors.shape[1]
    earlier = as_bf16(iota((n, n), 0) < iota((n, n), 1))
    ranks = []
    for k in range(ORBITALS):
        onehot = jnp.where(iota((LANES, n), 0) == sectors[k : k + 1, :], 1.0, 0.0)
        before = mm(onehot.astype(BF16), earlier)
        ranks.append(jnp.sum(before * onehot, axis=0, keepdims=True))
    return jnp.concatenate(
        [
            sectors.astype(F32),
            *ranks,
            outcomes.astype(F32) + 1.0,
            jnp.zeros((8 - 3 * ORBITALS, n), F32),
        ],
        axis=0,
    )


def fill_messages(send_ref, rows, k, table, columns):
    slots, n = send_ref.shape[0], rows.shape[0]
    first = table[SECTOR + k : SECTOR + k + 1, :] * MSG
    slot = first + table[RANK + k : RANK + k + 1, :]
    at = iota((slots, n), 0)
    data = mm(as_bf16(at == slot.astype(jnp.int32)), rows)
    send_ref[...] = data.astype(BF16)
    codes = as_bf16(
        iota((n, LANES), 1) == columns[:, RANK + k : RANK + k + 1].astype(jnp.int32),
        columns[:, CODE + k : CODE + k + 1],
    )
    heads = as_bf16(iota((LANES, n), 0) == table[SECTOR + k : SECTOR + k + 1, :].astype(jnp.int32))
    lines = mm(heads, codes)[: slots // MSG]
    in_head = iota((slots // MSG, MSG, LANES), 1) == CAP
    front = data[:, :LANES].reshape(slots // MSG, MSG, LANES)
    front = jnp.where(in_head, lines[:, None, :], front)
    send_ref[:, :LANES] = front.reshape(slots, LANES).astype(BF16)


def picked_rows(back, k, columns):
    slots, n = back.shape[0], columns.shape[0]
    slot = columns[:, SECTOR + k : SECTOR + k + 1] * MSG + columns[:, RANK + k : RANK + k + 1]
    return mm(as_bf16(iota((n, slots), 1) == slot.astype(jnp.int32)), back).astype(BF16)


def picked_probs(back, k, columns):
    slots, n = back.shape[0], columns.shape[0]
    messages = slots // MSG
    front = back[:, :LANES].astype(F32).reshape(messages, MSG, LANES)
    of = as_bf16(
        iota((n, messages), 1) == columns[:, SECTOR + k : SECTOR + k + 1].astype(jnp.int32)
    )
    here = iota((n, LANES), 1) == columns[:, RANK + k : RANK + k + 1].astype(jnp.int32)
    found = []
    for s in range(OUTCOMES):
        lines = mm(of, front[:, CAP + s, :].astype(BF16))
        found.append(jnp.sum(jnp.where(here, lines, 0.0), axis=1, keepdims=True))
    return found


def first_kernel(vec_ref, sec_ref, out_ref, send_ref, table_ref, columns_ref):
    table = index_table(sec_ref[...], out_ref[...])
    columns = table.T
    table_ref[...] = table
    columns_ref[...] = columns
    fill_messages(send_ref, vec_ref[...], 0, table, columns)


def middle_kernel(back_ref, table_ref, columns_ref, send_ref):
    columns = columns_ref[...]
    rows = picked_rows(back_ref[...], 0, columns)
    fill_messages(send_ref, rows, 1, table_ref[...], columns)


def probs_kernel(back_ref, columns_ref, probs_ref):
    columns = columns_ref[...]
    found = picked_probs(back_ref[...], 0, columns)
    probs_ref[...] = jnp.concatenate(found + found, axis=1)


def last_kernel(back_ref, columns_ref, probs0_ref, probs_ref, final_ref):
    columns, back = columns_ref[...], back_ref[...]
    final_ref[...] = picked_rows(back, 1, columns)
    found = jnp.concatenate(picked_probs(back, 1, columns), axis=1)
    both = jnp.concatenate([probs0_ref[:, :OUTCOMES], found], axis=1)
    probs_ref[...] = both.T.astype(BF16)


def row_and_part(place):
    return lax.div(place, PARTS), lax.rem(place, PARTS)


def pack_kernel(place_ref, first_ref, second_ref, rest_ref, *packed_refs):
    _, qs, ss, rs, lanes = first_ref.shape
    row, part = row_and_part(place_ref[0])
    odd = lax.rem(row, 2) == 1
    lane = iota((ss, rs, lanes), 2)
    low = lane < lanes // 2
    first_weight = jnp.where(low & jnp.logical_not(odd), 1.0, 2.0)
    second_weight = jnp.where(low | jnp.logical_not(odd), 2.0, 1.0)
    for d in range(qs):
        q = lax.rem(part + d, qs)
        parts = [
            (first_ref[0, q].astype(F32) * first_weight).reshape(ss * rs, lanes),
            (second_ref[0, q].astype(F32) * second_weight).reshape(ss * rs, lanes),
        ]
        rest = rest_ref[0, q].astype(F32)
        for s in range(0, ss, 2):
            one, two = rest[s], rest[s + 1]
            one = jnp.where(odd, pltpu.roll(one, lanes // 2, 1), one)
            two = jnp.where(odd, two, pltpu.roll(two, lanes // 2, 1))
            parts.append(jnp.where(low[0], one, two))
        packed_refs[d][...] = jnp.concatenate(parts, axis=0).astype(BF16)


def packed_blocks(place, environments, k):
    _, qs, ss, rs, cs = environments.shape
    line = (10 * rs, LANES)

    def at(index):
        def place_of(i, place):
            return (k, 0, 0, 0, lax.rem(index(row_and_part(place[0])[0]), 4))

        return pl.BlockSpec((1, qs, ss, rs, LANES), place_of)

    return pl.pallas_call(
        pack_kernel,
        out_shape=[shape(line, BF16)] * qs,
        grid_spec=pltpu.PrefetchScalarGridSpec(
            num_scalar_prefetch=1,
            grid=(1,),
            in_specs=[
                at(lambda z: lax.div(z + 1, 2)),
                at(lambda z: lax.div(z + 1, 2) + 1),
                at(lambda z: lax.div(z, 2) + 2 - 2 * lax.rem(z, 2)),
            ],
            out_specs=[pl.BlockSpec(line, lambda i, place: (0, 0))] * qs,
        ),
        compiler_params=pltpu.CompilerParams(vmem_limit_bytes=PACK_LIMIT),
    )(place, environments, environments, environments)


def unpack(part, blocks, env_ref):
    ds = 4
    rs = env_ref.shape[1] // (8 * ds)
    lane = iota((rs, LANES), 1)
    zero = jnp.zeros((rs, LANES), BF16)
    for z in range(8):
        odd, tile = z % 2, z // 2
        keep = (lane >= LANES // 2) if odd else (lane < LANES // 2)
        for d in range(ds):
            first = z * ds * rs + lax.rem(part + ds - d, ds) * rs
            rows = pl.ds(pl.multiple_of(first, rs), rs)
            block = blocks.at[z, d]

            def put(s, at, value):
                at %= 4
                env_ref[s, rows, at * LANES : (at + 1) * LANES] = value

            for s in range(OUTCOMES):
                put(s, tile + odd, block[s * rs : (s + 1) * rs, :])
                put(s, tile + odd + 1, block[(OUTCOMES + s) * rs : (OUTCOMES + s + 1) * rs, :])
                at = (2 * OUTCOMES + s // 2) * rs
                half = block[at : at + rs, :].astype(F32)
                if s % 2 != odd:
                    half = pltpu.roll(half, LANES // 2, 1)
                put(s, tile if odd else tile + 2, jnp.where(keep, half, 0.0).astype(BF16))
                put(s, tile + 3, zero)


def stage_kernel(
    k,
    place_ref,
    rows_ref,
    sites_hbm,
    packed_hbm,
    back_hbm,
    packed,
    site_ref,
    back_ref,
    env_ref,
    picked_ref,
    in_sems,
    out_sems,
):
    row, part = row_and_part(place_ref[0])
    slots, width = rows_ref.shape
    chunk = picked_ref.shape[0]
    gathered = pltpu.make_async_copy(packed_hbm, packed, in_sems.at[OUTCOMES])
    sites = [
        pltpu.make_async_copy(
            sites_hbm.at[k, part, :, width * s : width * (s + 1)], site_ref.at[s], in_sems.at[s]
        )
        for s in range(OUTCOMES)
    ]
    sites[0].start()
    gathered.start()
    for s in range(1, OUTCOMES):
        sites[s].start()

    messages = chunk // MSG
    cube = (messages, MSG, LANES)
    within = iota(cube, 1).reshape(chunk, LANES)
    diagonal = iota((chunk, LANES), 1) == within
    in_data = within[:, 0:1] < CAP
    sent = []
    for number, start in enumerate(range(0, slots, chunk)):
        at = slice(start, start + chunk)
        rows = rows_ref[at, :]
        front = rows[:, :LANES].astype(F32).reshape(cube)
        codes = jnp.broadcast_to(front[:, CAP : CAP + 1, :], cube).reshape(chunk, LANES)
        code = jnp.sum(jnp.where(diagonal, codes, 0.0), axis=1, keepdims=True)
        code = jnp.where(in_data, code, 0.0)
        weights = []
        for s in range(OUTCOMES):
            if number == 0:
                sites[s].wait()
            amplitudes = mm(rows, site_ref[s])
            if number == 0 and s == 0:
                gathered.wait()
                unpack(part, packed, env_ref)
            images = mm(amplitudes.astype(BF16), env_ref[s])
            weights.append(jnp.sum(images * amplitudes, axis=1, keepdims=True))
            chosen = code == (s + 1.0)
            if s == 0:
                picked_ref[...] = jnp.where(chosen, amplitudes, 0.0)
            else:
                picked_ref[...] = jnp.where(chosen, amplitudes, picked_ref[...])
        filled = code > 0.0
        total = jnp.where(filled, weights[0] + weights[1] + weights[2] + weights[3], 1.0)
        lines = jnp.zeros((chunk, LANES), F32)
        chosen_weight = jnp.ones((chunk, 1), F32)
        for s in range(OUTCOMES):
            prob = jnp.where(filled, weights[s] / total, 0.0)
            line = jnp.sum(jnp.where(diagonal, prob, 0.0).reshape(cube), axis=1, keepdims=True)
            line = jnp.broadcast_to(line, cube).reshape(chunk, LANES)
            lines = jnp.where(within == CAP + s, line, lines)
            chosen_weight = jnp.where(code == (s + 1.0), weights[s], chosen_weight)
        picked = picked_ref[...] * lax.rsqrt(chosen_weight / width)
        back_ref[at, :] = picked.astype(BF16)
        back_ref[at, :LANES] = jnp.where(in_data, picked[:, :LANES], lines).astype(BF16)
        copy = pltpu.make_async_copy(back_ref.at[at], back_hbm.at[at], out_sems.at[number])
        copy.start()
        sent.append(copy)
    for copy in sent:
        copy.wait()


def stage(k, place, rows, sites, packed):
    slots, width = rows.shape
    chunk = 16 * MSG
    count = len(packed)
    block = packed[0].shape[-3:]
    hbm, vmem = pl.BlockSpec(memory_space=pl.ANY), pl.BlockSpec(memory_space=pltpu.VMEM)
    return pl.pallas_call(
        functools.partial(stage_kernel, k),
        out_shape=shape((slots, width), BF16),
        in_specs=[pl.BlockSpec(memory_space=pltpu.SMEM), vmem, hbm, hbm],
        out_specs=hbm,
        scratch_shapes=[
            pltpu.VMEM(packed.shape, BF16),
            pltpu.VMEM((OUTCOMES, width, width), BF16),
            pltpu.VMEM((slots, width), BF16),
            pltpu.VMEM((OUTCOMES, width, width), BF16),
            pltpu.VMEM((chunk, width), F32),
            pltpu.SemaphoreType.DMA((OUTCOMES + 1,)),
            pltpu.SemaphoreType.DMA((slots // chunk,)),
        ],
        compiler_params=pltpu.CompilerParams(vmem_limit_bytes=VMEM_LIMIT),
    )(place, near(rows), sites, packed)


def local(vectors, sectors, outcomes, sites, environments):
    n, width = vectors.shape
    sector_total = sites.shape[1] * lax.axis_size("sector")
    slots = sector_total * MSG
    place = lax.axis_index(("row", "part")).astype(jnp.int32).reshape(1)

    def own_blocks(environments, k):
        blocks = packed_blocks(place, environments, k)
        blocks = [blocks[0]] + [
            lax.ppermute(blocks[d], "part", [(i, (i + d) % PARTS) for i in range(PARTS)])
            for d in range(1, PARTS)
        ]
        return jnp.stack(blocks)

    env0 = own_blocks(environments, 0)
    env0, environments = lax.optimization_barrier((env0, environments))
    env0 = lax.all_gather(env0, "row", axis=0)
    env1, vectors = lax.optimization_barrier((own_blocks(environments, 1), vectors))
    send, table, columns = call(
        first_kernel,
        (shape((slots, width), BF16), pltpu.VMEM((8, n), F32), pltpu.VMEM((n, 8), F32)),
        vectors,
        sectors.T,
        outcomes.T,
    )

    def exchanged(messages):
        messages = messages.reshape(sector_total, MSG, width)
        messages = lax.all_to_all(
            messages, ("sector", "part"), split_axis=0, concat_axis=0, tiled=True
        )
        return messages.reshape(slots, width)

    back = exchanged(send)
    env1, env0 = lax.optimization_barrier((env1, env0))
    env1 = lax.all_gather(env1, "row", axis=0)
    back = exchanged(stage(0, place, back, sites, env0))
    send = call(middle_kernel, shape((slots, width), BF16), back, table, columns)
    probs0 = call(probs_kernel, pltpu.VMEM((n, 8), F32), back, columns)
    back = exchanged(stage(1, place, exchanged(send), sites, env1))
    probs, final = call(
        last_kernel,
        (shape((ORBITALS * OUTCOMES, n), BF16), shape((n, width), BF16)),
        back,
        columns,
        probs0,
    )
    return (probs.T, final)


def solution(mesh):
    sector, section = mesh.devices.shape

    def whole(vectors, sectors, outcomes, sites, environments):
        fine = Mesh(
            mesh.devices.reshape(sector, section // PARTS, PARTS), ("sector", "row", "part")
        )
        split = P(("sector", "row", "part"), None)
        return jax.shard_map(
            local,
            mesh=fine,
            in_specs=(
                split,
                split,
                split,
                P(None, "sector", None, None),
                P(None, "sector", None, ("row", "part"), None),
            ),
            out_specs=(split, split),
            check_vma=False,
        )(vectors, sectors, outcomes, sites, environments)

    return whole
```
